32 devices in a mesh: freq: 8 (over z, x), tmpl: 4 (over y, core).
Axes of the slice: x: 2, y: 2, z: 4, core: 2. Of those that a mesh axis runs over, the one named last changes fastest.
Arguments:
- strain: bfloat16 [2, 16, 2097152], P(None, 'tmpl', 'freq'), may hold values from -6 to 6
- fiducial: bfloat16 [2, 16, 2097152], P(None, 'tmpl', 'freq'), may hold values from -6 to 6
- psd: float32 [16, 2097152], P('tmpl', 'freq'), may hold values from 0.25 to 8
- time_shift: float32 [16], P('tmpl'), may hold values from -8 to 8
- phase_shift: float32 [16], P('tmpl'), may hold values from -3.140625 to 3.140625
- bin_blocks: int32 [8, 32], replicated, may hold values from 1 to 128, as said below
- bin_owner: int32 [8, 32], replicated, may hold values from 0 to 7, as said below
Outputs:
- moved: bfloat16 [2, 16, 256, 16384], P(None, 'tmpl', 'freq')
- summary: float32 [6, 16, 256], P(None, 'tmpl', 'freq')
The draws below stay inside these ranges and needn't reach their ends.
Inputs may be any that keep to these rules, and one draw needn't show every extreme that they name: `bin_owner`: row p lists, in frequency order, the owners of the bins in the frequencies of index p of freq; each row names every owner exactly 4 times. `bin_blocks`: row p holds, in frequency order, the lengths in blocks of the bins in the frequencies of index p of freq; the 4 bins that row p hands to one owner total 2 * 128 blocks, and some bin of each row is 128 blocks long.
All inputs are finite; a program needn't handle non-finite values.
Results may differ from the reference program's by a relative error of at most 0.001.
The reference program's roundings to bfloat16 on the way (of `product`, `power` and `power_slots`) count: a program that leaves them out, or rounds other values in their place, can miss the bound.
Values may be sent and summed in bfloat16 or wider, within the bound.
A program may use at most 128 MiB of HBM per device.

```python
import math
import jax
import jax.numpy as jnp

PAIR_BINS = 4
BINS_DEV = 32
BLK_DEV = 2048
MOST = 128
FREQS = 2097152
ROWS = 16
NBINS = 256
N_FREQ = 8


def binning_tables(key):

    def one_row(position):
        row_key = jax.random.fold_in(key, position + 7)
        owners = (jax.random.permutation(jax.random.fold_in(row_key, 1), BINS_DEV) % N_FREQ).astype(jnp.int32)
        forced = jax.random.randint(jax.random.fold_in(row_key, 2), (), 0, N_FREQ)
        keys = jax.random.split(jax.random.fold_in(row_key, 3), 5)
        groups = jnp.arange(N_FREQ, dtype=jnp.int32)
        is_forced = groups == forced
        drawn_total = jax.random.randint(keys[0], (N_FREQ,), 2, 2 * MOST - 1)
        heavy_total = jax.random.randint(keys[1], (N_FREQ,), MOST + 1, 2 * MOST - 1)
        first_total = jnp.where(is_forced, heavy_total, drawn_total)
        first = jax.random.randint(keys[2], (N_FREQ,), jnp.maximum(1, first_total - MOST), jnp.minimum(MOST, first_total - 1) + 1)
        first = jnp.where(is_forced, MOST, first)
        second = first_total - first
        rest = 2 * MOST - first_total
        third = jax.random.randint(keys[3], (N_FREQ,), jnp.maximum(1, rest - MOST), jnp.minimum(MOST, rest - 1) + 1)
        fourth = rest - third
        stacked = jnp.stack([first, second, third, fourth], axis=1).astype(jnp.int32)
        order = jax.vmap(lambda sub: jax.random.permutation(sub, 4))(jax.random.split(keys[4], N_FREQ))
        stacked = jnp.take_along_axis(stacked, order.astype(jnp.int32), axis=1)
        position_ids = jnp.arange(BINS_DEV, dtype=jnp.int32)
        earlier = position_ids[None, :] < position_ids[:, None]
        same = owners[:, None] == owners[None, :]
        ranks = jnp.sum(jnp.logical_and(same, earlier).astype(jnp.int32), axis=1)
        lengths = stacked[owners, ranks]
        return (owners, lengths.astype(jnp.int32))
    return jax.vmap(one_row)(jnp.arange(N_FREQ, dtype=jnp.int32))


def draw_bin_owner(key, part):
    owners, lengths = binning_tables(jax.random.fold_in(key, 11))
    return owners.astype(jnp.int32)


def draw_bin_blocks(key, part):
    owners, lengths = binning_tables(jax.random.fold_in(key, 11))
    return lengths.astype(jnp.int32)


def shard_levels(own_key, dims, cuts, smallest, high):
    loudness, own = 1.0, jax.random.fold_in(own_key, 6)
    for dim, parts in cuts:
        draws = jnp.exp(jax.random.uniform(jax.random.fold_in(own, dim), (parts,), jnp.float32, smallest / len(cuts), high / len(cuts)))
        loudness = loudness * jnp.repeat(draws, dims[dim] // parts).reshape([-1 if axis == dim else 1 for axis in range(len(dims))])
    return loudness


def scatter_about(rng, dims, scale, bound, shards=(), kind=jnp.bfloat16):
    values = scale * jax.random.normal(rng, dims, jnp.float32)
    if shards:
        values = values * shard_levels(rng, dims, shards, -0.22, 0.18)
    return jnp.clip(values, -bound, bound).astype(kind)


def setup_inputs(seed: int = 0) -> dict:
    splits = jax.random.split(jax.random.key(seed), 8)
    return {
        "strain": scatter_about(splits[0], (2, ROWS, FREQS), 1.0, 6.0, ((1, 4), (2, 8))),
        "fiducial": scatter_about(splits[1], (2, ROWS, FREQS), 1.0, 6.0, ((1, 4), (2, 8))),
        "psd": jnp.clip(jnp.exp(math.log(8.0) - 3.465736 * jax.random.uniform(splits[2], (ROWS, FREQS), jnp.float32) ** shard_levels(splits[2], (ROWS, FREQS), ((0, 4), (1, 8)), -0.2, 0.2)), 0.25, 8.0),
        "time_shift": jnp.clip(jax.random.uniform(splits[3], (ROWS,), jnp.float32, -8.0, 8.0) * shard_levels(splits[3], (ROWS,), ((0, 4),), -0.4, 0.0), -8.0, 8.0),
        "phase_shift": jnp.clip(jax.random.uniform(splits[4], (ROWS,), jnp.float32, -3.140625, 3.140625), -3.140625, 3.140625),
        "bin_blocks": draw_bin_blocks(jax.random.fold_in(splits[7], 71), 0),
        "bin_owner": draw_bin_owner(jax.random.fold_in(splits[7], 71), 0),
    }


two_pi = 2.0 * math.pi
ratio_scale = 1.0 / 64.0
power_scale = 1.0 / 2048.0


def heterodyne(strain, fiducial, weight, time_shift, phase_shift, unit):
    strain_re = strain[0].astype(jnp.float32)
    strain_im = strain[1].astype(jnp.float32)
    fid_re = fiducial[0].astype(jnp.float32)
    fid_im = fiducial[1].astype(jnp.float32)
    angle = (two_pi * time_shift)[:, None] * unit[None, :] + phase_shift[:, None]
    cosine = jnp.cos(angle)
    sine_val = jnp.sin(angle)
    cross_re = strain_re * fid_re + strain_im * fid_im
    cross_im = strain_im * fid_re - strain_re * fid_im
    prod_re = weight * (cross_re * cosine + cross_im * sine_val)
    prod_im = weight * (cross_im * cosine - cross_re * sine_val)
    product = jnp.stack([prod_re, prod_im]).astype(jnp.bfloat16)
    power = (weight * (fid_re * fid_re + fid_im * fid_im)).astype(jnp.bfloat16)
    return product, power


def slot_tables(bin_blocks, bin_owner):
    count = bin_blocks.shape[1]
    starts = jnp.cumsum(bin_blocks, axis=1).astype(jnp.int32) - bin_blocks
    position = jnp.arange(count, dtype=jnp.int32)
    earlier = position[None, :] < position[:, None]
    same = bin_owner[:, :, None] == bin_owner[:, None, :]
    ranks = jnp.sum(jnp.logical_and(same, earlier[None]).astype(jnp.int32), axis=2)
    return starts, ranks


def arrange(values, first_block, lengths, most_blocks):
    lead = values.shape[:-1]
    blocks = values.shape[-1] // 128
    tiled = values.reshape(lead + (blocks, 128))
    step_ids = jnp.arange(most_blocks, dtype=jnp.int32)
    block_ids = jnp.minimum(first_block[:, None] + step_ids[None, :], blocks - 1)
    picked = jnp.take(tiled, block_ids.reshape(-1), axis=values.ndim - 1)
    slot_count = first_block.shape[0]
    picked = picked.reshape(lead + (slot_count, most_blocks, 128))
    live = (step_ids[None, :] < lengths[:, None])[:, :, None]
    picked = jnp.where(live, picked, jnp.zeros((), values.dtype))
    return picked.reshape(lead + (slot_count, most_blocks * 128))


def summarize(moved, power_slots, lengths):
    width = moved.shape[-1]
    offset = (jnp.arange(width, dtype=jnp.int32).astype(jnp.float32)[None, :] + 0.5
              - 64.0 * lengths.astype(jnp.float32)[:, None]) / 128.0
    values = moved.astype(jnp.float32)
    weighted = power_slots[0].astype(jnp.float32)
    plain_sum = jnp.sum(values, axis=-1) * ratio_scale
    slope_sum = jnp.sum(values * offset, axis=-1) * ratio_scale
    power_sum = jnp.sum(weighted, axis=-1) * power_scale
    power_slope = jnp.sum(weighted * offset, axis=-1) * power_scale
    return jnp.concatenate([plain_sum, slope_sum, power_sum[None], power_slope[None]], axis=0)


def reference(strain, fiducial, psd, time_shift, phase_shift, bin_blocks, bin_owner):
    padded = jnp.pad(psd, ((0, 0), (1, 1)))
    weight = 1.0 / (0.25 * (padded[:, :-2] + 2.0 * padded[:, 1:-1] + padded[:, 2:]))
    unit = jnp.arange(FREQS, dtype=jnp.int32).astype(jnp.float32) / FREQS
    product, power = heterodyne(strain, fiducial, weight, time_shift, phase_shift, unit)
    starts, ranks = slot_tables(bin_blocks, bin_owner)
    source = jnp.arange(N_FREQ, dtype=jnp.int32)[:, None]
    slots = (bin_owner * BINS_DEV + source * PAIR_BINS + ranks).reshape(-1)
    first_block = jnp.zeros((NBINS,), jnp.int32).at[slots].set((source * BLK_DEV + starts).reshape(-1))
    lengths = jnp.zeros((NBINS,), jnp.int32).at[slots].set(bin_blocks.reshape(-1))
    moved = arrange(product, first_block, lengths, MOST)
    power_slots = arrange(power, first_block, lengths, MOST)[None]
    summary = summarize(moved, power_slots, lengths)
    return moved, summary
```

```python
import functools
import math

import jax
import jax.numpy as jnp
from jax import lax
from jax.experimental import pallas as pl
from jax.experimental.pallas import tpu as pltpu
from jax.sharding import PartitionSpec as P

two_pi = 2.0 * math.pi
ratio_scale = 1.0 / 64.0
power_scale = 1.0 / 2048.0
LANES = 128
SUB = 32
TABLE = 256


def het_kernel(strain, fid, psd, prev, nxt, halo, cos_t, sin_t, cos_s, sin_s, prod, sums, pad, power):
    rows = psd.shape[0]
    step, last = pl.program_id(0), pl.num_programs(0) - 1
    pad[8 : 8 + rows] = psd[...]
    pad[0:8] = jnp.where(step == 0, halo[0], prev[...])
    pad[8 + rows : 16 + rows] = jnp.where(step == last, halo[1], nxt[...])
    lane = lax.broadcasted_iota(jnp.int32, (SUB, LANES), 1)
    fold = (SUB // 8, 8, LANES)

    for outer in range(rows // TABLE):
        cs, ss = cos_s[outer][None], sin_s[outer][None]

        def inner(i, carry, outer=outer, cs=cs, ss=ss):
            off = pl.multiple_of(i * SUB, SUB)
            at = pl.multiple_of(outer * TABLE + i * SUB, SUB)
            x = pad[pl.ds(at + 8, SUB)]
            before = pltpu.roll(jnp.where(lane == LANES - 1, pad[pl.ds(at + 4, SUB)], x), 1, 1)
            after = pltpu.roll(jnp.where(lane == 0, pad[pl.ds(at + 12, SUB)], x), LANES - 1, 1)
            weight = 1.0 / (0.25 * (before + 2.0 * x + after))
            ct = cos_t[pl.ds(off, SUB)].reshape(fold)
            st = sin_t[pl.ds(off, SUB)].reshape(fold)
            cosine = (ct * cs - st * ss).reshape(SUB, LANES)
            sine = (st * cs + ct * ss).reshape(SUB, LANES)
            s_re = strain[0, pl.ds(at, SUB)].astype(jnp.float32)
            s_im = strain[1, pl.ds(at, SUB)].astype(jnp.float32)
            f_re = fid[0, pl.ds(at, SUB)].astype(jnp.float32)
            f_im = fid[1, pl.ds(at, SUB)].astype(jnp.float32)
            cross_re = s_re * f_re + s_im * f_im
            cross_im = s_im * f_re - s_re * f_im
            prod[0, pl.ds(at, SUB)] = (weight * (cross_re * cosine + cross_im * sine)).astype(jnp.bfloat16)
            prod[1, pl.ds(at, SUB)] = (weight * (cross_im * cosine - cross_re * sine)).astype(jnp.bfloat16)
            power[pl.ds(at, SUB)] = (weight * (f_re * f_re + f_im * f_im)).astype(jnp.bfloat16)
            return carry

        lax.fori_loop(0, TABLE // SUB, inner, 0)

    row = lax.broadcasted_iota(jnp.int32, (8, LANES), 0)
    col = lax.broadcasted_iota(jnp.int32, (8, LANES), 1).astype(jnp.float32)
    total = jnp.zeros((8, rows), jnp.float32)
    for q, values in enumerate((prod[0], prod[1], power[...])):
        w = jnp.where(row == 2 * q, 1.0, jnp.where(row == 2 * q + 1, (col + 0.5) / 128.0, 0.0))
        total += lax.dot_general(
            w.astype(jnp.bfloat16), values, (((1,), (1,)), ((), ())),
            preferred_element_type=jnp.float32,
        )
    sums[...] = total


def heterodyne(strain, fid, psd, halo, cos_t, sin_t, cos_s, sin_s):
    total = psd.shape[0]
    rows = min(1024, total)
    steps = total // rows
    per = rows // 8
    return pl.pallas_call(
        het_kernel,
        grid=(steps,),
        in_specs=[
            pl.BlockSpec((2, rows, LANES), lambda i: (0, i, 0)),
            pl.BlockSpec((2, rows, LANES), lambda i: (0, i, 0)),
            pl.BlockSpec((rows, LANES), lambda i: (i, 0)),
            pl.BlockSpec((8, LANES), lambda i: (jnp.maximum(i * per - 1, 0), 0)),
            pl.BlockSpec((8, LANES), lambda i: (jnp.minimum((i + 1) * per, steps * per - 1), 0)),
            pl.BlockSpec((2, 8, LANES), lambda i: (0, 0, 0)),
            pl.BlockSpec((TABLE, LANES), lambda i: (0, 0)),
            pl.BlockSpec((TABLE, LANES), lambda i: (0, 0)),
            pl.BlockSpec((rows // TABLE, 8, LANES), lambda i: (i, 0, 0)),
            pl.BlockSpec((rows // TABLE, 8, LANES), lambda i: (i, 0, 0)),
        ],
        out_specs=[
            pl.BlockSpec((2, rows, LANES), lambda i: (0, i, 0)),
            pl.BlockSpec((8, rows), lambda i: (0, i)),
        ],
        out_shape=[
            jax.ShapeDtypeStruct((2, total, LANES), jnp.bfloat16),
            jax.ShapeDtypeStruct((8, total), jnp.float32),
        ],
        scratch_shapes=[
            pltpu.VMEM((rows + 16, LANES), jnp.float32),
            pltpu.VMEM((rows, LANES), jnp.bfloat16),
        ],
        name="heterodyne",
    )(strain, fid, psd, psd, psd, halo, cos_t, sin_t, cos_s, sin_s)


def pack_kernel(starts, lengths, owners, offsets, prod, packed, sem):
    bins = starts.shape[0]

    def copy(j, c):
        n = lengths[j]
        return pltpu.make_async_copy(
            prod.at[c, pl.ds(starts[j], n)],
            packed.at[owners[j], c, pl.ds(offsets[j], n)],
            sem.at[2 * j + c],
        )

    def start(j, carry):
        copy(j, 0).start()
        copy(j, 1).start()
        return carry

    def wait(j, carry):
        copy(j, 0).wait()
        copy(j, 1).wait()
        return carry

    lax.fori_loop(0, bins, start, 0)
    lax.fori_loop(0, bins, wait, 0)


def pack(starts, lengths, owners, offsets, prod, groups, span):
    return pl.pallas_call(
        pack_kernel,
        grid_spec=pltpu.PrefetchScalarGridSpec(
            num_scalar_prefetch=4,
            in_specs=[pl.BlockSpec(memory_space=pltpu.VMEM)],
            out_specs=pl.BlockSpec(memory_space=pl.ANY),
            scratch_shapes=[pltpu.SemaphoreType.DMA((2 * starts.shape[0],))],
        ),
        out_shape=jax.ShapeDtypeStruct((groups, 2, span) + prod.shape[2:], jnp.bfloat16),
        name="pack",
    )(starts, lengths, owners, offsets, prod)


def unpack_kernel(chunk, pair, lengths, offsets, got, out, work):
    group, m0 = pl.program_id(1), pl.program_id(2) * chunk
    span, rows = got.shape[2], got.shape[3]
    slots = out.shape[2]
    for s in range(slots):
        slot = group * slots + s
        n = lengths[slot] - m0
        base = offsets[slot] + m0

        @pl.when(n > 0)
        def _(s=s, n=n, base=base):
            for m in range(chunk):
                value = got[s // pair, 0, jnp.minimum(base + m, span - 1)].astype(jnp.float32)
                value = jnp.where(m < n, value, 0.0)
                work[m, pl.ds(s, rows, stride=slots)] = value

        @pl.when(n <= 0)
        def _(s=s):
            for m in range(chunk):
                work[m, pl.ds(s, rows, stride=slots)] = jnp.zeros((rows, LANES), jnp.float32)

    for m in range(chunk):
        for r in range(rows):
            out[0, r, :, m * LANES : (m + 1) * LANES] = work[m, r * slots : (r + 1) * slots].astype(jnp.bfloat16)


def unpack(lengths, offsets, got, pair, most):
    groups, _, span, rows, _ = got.shape
    bins = groups * pair
    slots = min(16, bins)
    chunk = min(16, most)
    return pl.pallas_call(
        functools.partial(unpack_kernel, chunk, pair),
        grid_spec=pltpu.PrefetchScalarGridSpec(
            num_scalar_prefetch=2,
            grid=(2, bins // slots, most // chunk),
            in_specs=[
                pl.BlockSpec((slots // pair, 1, span, rows, LANES), lambda c, g, m, *_: (g, c, 0, 0, 0))
            ],
            out_specs=pl.BlockSpec((1, rows, slots, chunk * LANES), lambda c, g, m, *_: (c, 0, g, m)),
            scratch_shapes=[pltpu.VMEM((chunk, rows * slots, LANES), jnp.float32)],
        ),
        out_shape=jax.ShapeDtypeStruct((2, rows, bins, most * LANES), jnp.bfloat16),
        name="unpack",
    )(lengths, offsets, got)


def local(strain, fiducial, psd, time_shift, phase_shift, bin_blocks, bin_owner):
    n_freq = lax.axis_size("freq")
    me = lax.axis_index("freq")
    rows, width = psd.shape
    blocks = width // LANES
    bins = bin_blocks.shape[1]
    pair = bins // n_freq
    most = 2 * blocks // bins
    span = 2 * most

    strain_v = strain.reshape(2, rows, blocks, LANES).transpose(0, 2, 1, 3).reshape(2, blocks * rows, LANES)
    fid_v = fiducial.reshape(2, rows, blocks, LANES).transpose(0, 2, 1, 3).reshape(2, blocks * rows, LANES)
    psd_v = psd.reshape(rows, blocks, LANES).transpose(1, 0, 2).reshape(blocks * rows, LANES)

    up = [(i, i + 1) for i in range(n_freq - 1)]
    down = [(i + 1, i) for i in range(n_freq - 1)]
    halo = jnp.stack([lax.ppermute(psd_v[-8:], "freq", up), lax.ppermute(psd_v[:8], "freq", down)])

    rate = two_pi * time_shift
    total = width * n_freq
    table_blocks = TABLE // rows
    inside = jnp.arange(table_blocks * LANES, dtype=jnp.int32).astype(jnp.float32).reshape(table_blocks, 1, LANES) / total
    inside = (rate[None, :, None] * inside).reshape(TABLE, LANES)
    first = me * width + jnp.arange(blocks // table_blocks, dtype=jnp.int32) * (table_blocks * LANES)
    outer = rate[None, :] * (first.astype(jnp.float32) / total)[:, None] + phase_shift[None, :]
    spread = lambda v: jnp.broadcast_to(jnp.tile(v, (1, 8 // rows))[:, :, None], (v.shape[0], 8, LANES))
    prod, sums = heterodyne(
        strain_v, fid_v, psd_v, halo,
        jnp.cos(inside), jnp.sin(inside), spread(jnp.cos(outer)), spread(jnp.sin(outer)),
    )

    position = jnp.arange(bins, dtype=jnp.int32)
    earlier = (position[None, :] < position[:, None])[None]
    same = bin_owner[:, :, None] == bin_owner[:, None, :]
    both = jnp.logical_and(same, earlier)
    starts = jnp.sum(jnp.where(earlier, bin_blocks[:, None, :], 0), axis=2)
    ranks = jnp.sum(both.astype(jnp.int32), axis=2)
    offsets = jnp.sum(jnp.where(both, bin_blocks[:, None, :], 0), axis=2)
    at_me = lambda a: lax.dynamic_index_in_dim(a, me, 0, keepdims=False)
    my_start, my_len, my_owner, my_off, my_rank = map(at_me, (starts, bin_blocks, bin_owner, offsets, ranks))
    packed = pack(my_start, my_len, my_owner, my_off, prod.reshape(2, blocks, rows, LANES), n_freq, span)

    got = lax.all_to_all(packed, "freq", split_axis=0, concat_axis=0, tiled=True)

    to_me = jnp.logical_and(
        (bin_owner == me)[:, None, :], ranks[:, None, :] == jnp.arange(pair, dtype=jnp.int32)[None, :, None]
    )
    in_len = jnp.sum(jnp.where(to_me, bin_blocks[:, None, :], 0), axis=2).reshape(-1)
    in_off = jnp.sum(jnp.where(to_me, offsets[:, None, :], 0), axis=2).reshape(-1)
    moved = unpack(in_len, in_off, got, pair, most)

    my_slot = my_owner * pair + my_rank
    hot = my_slot[None, :] == position[:, None]
    slot_first = jnp.sum(jnp.where(hot, my_start[None, :], 0), axis=1)
    slot_len = jnp.sum(jnp.where(hot, my_len[None, :], 0), axis=1)
    ids = jnp.arange(blocks, dtype=jnp.int32)
    rel = ids[None, :] - slot_first[:, None]
    live = jnp.logical_and(rel >= 0, rel < slot_len[:, None])
    centre = rel.astype(jnp.float32) - 0.5 * slot_len.astype(jnp.float32)[:, None]
    mask = jnp.where(live, 1.0, 0.0)
    tilt = jnp.where(live, centre, 0.0)
    parts = sums[:6].reshape(3, 2, blocks, rows)
    dot = functools.partial(jnp.einsum, precision=lax.Precision.HIGHEST)
    plain = dot("qbr,sb->qrs", parts[:, 0], mask)
    slope = dot("qbr,sb->qrs", parts[:, 1], mask) + dot("qbr,sb->qrs", parts[:, 0], tilt)
    local_summary = jnp.concatenate(
        [plain[:2] * ratio_scale, slope[:2] * ratio_scale, plain[2:] * power_scale, slope[2:] * power_scale]
    )
    summary = lax.all_to_all(local_summary, "freq", split_axis=2, concat_axis=2, tiled=True)
    return (moved, summary)


def solution(mesh):
    return jax.shard_map(
        local,
        mesh=mesh,
        in_specs=(
            P(None, "tmpl", "freq"),
            P(None, "tmpl", "freq"),
            P("tmpl", "freq"),
            P("tmpl"),
            P("tmpl"),
            P(),
            P(),
        ),
        out_specs=(P(None, "tmpl", "freq", None), P(None, "tmpl", "freq")),
        check_vma=False,
    )
```

```python
import functools
import math

import jax
import jax.numpy as jnp
from jax import lax
from jax.experimental import pallas as pl
from jax.experimental.pallas import tpu as pltpu
from jax.sharding import PartitionSpec as P


two_pi = 2.0 * math.pi
ratio_scale = 1.0 / 64.0
power_scale = 1.0 / 2048.0
LANES = 128
SUB = 32
TABLE = 256


def het_kernel(strain, fid, psd, prev, nxt, halo, cos_t, sin_t, cos_s, sin_s, real, imag, power, pad):
    rows = psd.shape[0]
    step, last = pl.program_id(0), pl.num_programs(0) - 1
    pad[8 : 8 + rows] = psd[...]
    pad[0:8] = jnp.where(step == 0, halo[0], prev[...])
    pad[8 + rows : 16 + rows] = jnp.where(step == last, halo[1], nxt[...])
    lane = lax.broadcasted_iota(jnp.int32, (SUB, LANES), 1)
    fold = (SUB // 8, 8, LANES)

    for outer in range(rows // TABLE):
        cs, ss = cos_s[outer][None], sin_s[outer][None]

        def inner(i, carry, outer=outer, cs=cs, ss=ss):
            off = pl.multiple_of(i * SUB, SUB)
            at = pl.multiple_of(outer * TABLE + i * SUB, SUB)
            x = pad[pl.ds(at + 8, SUB)]
            before = pltpu.roll(jnp.where(lane == LANES - 1, pad[pl.ds(at + 4, SUB)], x), 1, 1)
            after = pltpu.roll(jnp.where(lane == 0, pad[pl.ds(at + 12, SUB)], x), LANES - 1, 1)
            weight = 1.0 / (0.25 * (before + 2.0 * x + after))
            ct = cos_t[pl.ds(off, SUB)].reshape(fold)
            st = sin_t[pl.ds(off, SUB)].reshape(fold)
            cosine = (ct * cs - st * ss).reshape(SUB, LANES)
            sine = (st * cs + ct * ss).reshape(SUB, LANES)
            s_re = strain[0, pl.ds(at, SUB)].astype(jnp.float32)
            s_im = strain[1, pl.ds(at, SUB)].astype(jnp.float32)
            f_re = fid[0, pl.ds(at, SUB)].astype(jnp.float32)
            f_im = fid[1, pl.ds(at, SUB)].astype(jnp.float32)
            cross_re = s_re * f_re + s_im * f_im
            cross_im = s_im * f_re - s_re * f_im
            real[pl.ds(at, SUB)] = (weight * (cross_re * cosine + cross_im * sine)).astype(jnp.bfloat16)
            imag[pl.ds(at, SUB)] = (weight * (cross_im * cosine - cross_re * sine)).astype(jnp.bfloat16)
            power[pl.ds(at, SUB)] = (weight * (f_re * f_re + f_im * f_im)).astype(jnp.bfloat16)
            return carry

        lax.fori_loop(0, TABLE // SUB, inner, 0)


def heterodyne(strain, fid, psd, halo, cos_t, sin_t, cos_s, sin_s):
    total = psd.shape[0]
    rows = min(1024, total)
    steps = total // rows
    per = rows // 8
    return pl.pallas_call(
        het_kernel,
        grid=(steps,),
        in_specs=[
            pl.BlockSpec((2, rows, LANES), lambda i: (0, i, 0)),
            pl.BlockSpec((2, rows, LANES), lambda i: (0, i, 0)),
            pl.BlockSpec((rows, LANES), lambda i: (i, 0)),
            pl.BlockSpec((8, LANES), lambda i: (jnp.maximum(i * per - 1, 0), 0)),
            pl.BlockSpec((8, LANES), lambda i: (jnp.minimum((i + 1) * per, steps * per - 1), 0)),
            pl.BlockSpec((2, 8, LANES), lambda i: (0, 0, 0)),
            pl.BlockSpec((TABLE, LANES), lambda i: (0, 0)),
            pl.BlockSpec((TABLE, LANES), lambda i: (0, 0)),
            pl.BlockSpec((rows // TABLE, 8, LANES), lambda i: (i, 0, 0)),
            pl.BlockSpec((rows // TABLE, 8, LANES), lambda i: (i, 0, 0)),
        ],
        out_specs=[pl.BlockSpec((rows, LANES), lambda i: (i, 0))] * 3,
        out_shape=[jax.ShapeDtypeStruct((total, LANES), jnp.bfloat16)] * 3,
        scratch_shapes=[pltpu.VMEM((rows + 16, LANES), jnp.float32)],
        cost_estimate=pl.CostEstimate(flops=60 * total * LANES, bytes_accessed=18 * total * LANES, transcendentals=0),
        name="heterodyne",
    )(strain, fid, psd, psd, psd, halo, cos_t, sin_t, cos_s, sin_s)


def sums_kernel(tmpl_rows, real, imag, power, first, length, flat, tilted):
    rows = real.shape[0]
    cols = flat.shape[1]
    step = pl.program_id(0)
    row = lax.broadcasted_iota(jnp.int32, (8, LANES), 0)
    col = lax.broadcasted_iota(jnp.int32, (8, LANES), 1).astype(jnp.float32)
    lanes = jnp.zeros((8, rows), jnp.float32)
    for q, values in enumerate((real, imag, power)):
        w = jnp.where(row == 2 * q, 1.0, jnp.where(row == 2 * q + 1, (col + 0.5) / 128.0, 0.0))
        lanes += lax.dot_general(
            w.astype(jnp.bfloat16), values[...], (((1,), (1,)), ((), ())),
            preferred_element_type=jnp.float32,
        )
    index = lax.broadcasted_iota(jnp.int32, (rows, cols), 0)
    slot_row = lax.broadcasted_iota(jnp.int32, (rows, cols), 1) // (cols // tmpl_rows)
    rel = step * (rows // tmpl_rows) + index // tmpl_rows - first[...]
    live = (index % tmpl_rows == slot_row) & (rel >= 0) & (rel < length[...])
    mask = jnp.where(live, 1.0, 0.0)
    tilt = jnp.where(live, rel.astype(jnp.float32) - 0.5 * length[...].astype(jnp.float32), 0.0)

    @pl.when(step == 0)
    def _():
        flat[...] = jnp.zeros_like(flat)
        tilted[...] = jnp.zeros_like(tilted)

    dot = functools.partial(jnp.dot, precision=lax.Precision.HIGHEST, preferred_element_type=jnp.float32)
    flat[...] += dot(lanes, mask)
    tilted[...] += dot(lanes, tilt)


def bin_sums(tmpl_rows, real, imag, power, first, length):
    total = real.shape[0]
    rows = min(1024, total)
    cols = first.shape[1]
    block = pl.BlockSpec((rows, LANES), lambda i: (i, 0))
    table = pl.BlockSpec((1, cols), lambda i: (0, 0))
    return pl.pallas_call(
        functools.partial(sums_kernel, tmpl_rows),
        grid=(total // rows,),
        in_specs=[block, block, block, table, table],
        out_specs=[pl.BlockSpec((8, cols), lambda i: (0, 0))] * 2,
        out_shape=[jax.ShapeDtypeStruct((8, cols), jnp.float32)] * 2,
        cost_estimate=pl.CostEstimate(flops=200 * total * LANES, bytes_accessed=6 * total * LANES, transcendentals=0),
        name="sums",
    )(real, imag, power, first, length)


def pack_kernel(starts, lengths, offsets, prod, *rest):
    *packed, sem = rest
    pair = starts.shape[0] // len(packed)

    def copies():
        for step, target in enumerate(packed):
            for rank in range(pair):
                j = step * pair + rank
                n = lengths[j]
                yield pltpu.make_async_copy(
                    prod.at[pl.ds(starts[j], n)], target.at[pl.ds(offsets[j], n)], sem.at[j]
                )

    for copy in copies():
        copy.start()
    for copy in copies():
        copy.wait()


def pack(starts, lengths, offsets, prod, groups, span):
    shape = jax.ShapeDtypeStruct((span,) + prod.shape[1:], jnp.bfloat16)
    return pl.pallas_call(
        pack_kernel,
        grid_spec=pltpu.PrefetchScalarGridSpec(
            num_scalar_prefetch=3,
            in_specs=[pl.BlockSpec(memory_space=pltpu.VMEM)],
            out_specs=[pl.BlockSpec(memory_space=pl.ANY)] * groups,
            scratch_shapes=[pltpu.SemaphoreType.DMA((starts.shape[0],))],
        ),
        out_shape=[shape] * groups,
        cost_estimate=pl.CostEstimate(flops=0, bytes_accessed=4 * prod.size, transcendentals=0),
        name="pack",
    )(starts, lengths, offsets, prod)


def unpack_kernel(chunk, pair, unit, where, lengths, offsets, near, far, *rest):
    out, work = rest[-2:]
    m0 = pl.program_id(0) * chunk
    span, rows = near.shape[0], near.shape[1]
    slots = out.shape[2]
    for half, got in enumerate((near, far)):
        base_slot = (where[1] ^ half) * pair
        for rank in range(pair):
            j = (2 * unit + half) * pair + rank
            n = lengths[j] - m0
            base = offsets[j] + m0
            lane = base_slot + rank

            @pl.when(n > 0)
            def _(got=got, n=n, base=base, lane=lane):
                for m in range(chunk):
                    value = got[jnp.minimum(base + m, span - 1)].astype(jnp.float32)
                    value = jnp.where(m < n, value, 0.0)
                    work[m, pl.ds(lane, rows, stride=slots)] = value

            @pl.when(n <= 0)
            def _(lane=lane):
                for m in range(chunk):
                    work[m, pl.ds(lane, rows, stride=slots)] = jnp.zeros((rows, LANES), jnp.float32)

    for m in range(chunk):
        for r in range(rows):
            out[0, r, :, m * LANES : (m + 1) * LANES] = work[m, r * slots : (r + 1) * slots].astype(jnp.bfloat16)


def unpack(part, unit, where, lengths, offsets, near, far, dest, bins, pair, most):
    span, rows, _ = near.shape
    slots = 2 * pair
    chunk = min(16, most)
    whole = pl.BlockSpec((span, rows, LANES), lambda m, *_: (0, 0, 0))
    extra = [] if dest is None else [dest]
    size = rows * slots * most * LANES
    return pl.pallas_call(
        functools.partial(unpack_kernel, chunk, pair, unit),
        grid_spec=pltpu.PrefetchScalarGridSpec(
            num_scalar_prefetch=3,
            grid=(most // chunk,),
            in_specs=[whole, whole] + [pl.BlockSpec(memory_space=pl.ANY)] * len(extra),
            out_specs=pl.BlockSpec(
                (1, rows, slots, chunk * LANES), lambda m, w, *_: (part, 0, w[0] ^ unit, m)
            ),
            scratch_shapes=[pltpu.VMEM((chunk, rows * slots, LANES), jnp.float32)],
        ),
        out_shape=jax.ShapeDtypeStruct((2, rows, bins, most * LANES), jnp.bfloat16),
        input_output_aliases={5: 0} if extra else {},
        cost_estimate=pl.CostEstimate(flops=8 * size, bytes_accessed=3 * size, transcendentals=0),
        name="unpack",
    )(where, lengths, offsets, near, far, *extra)


def local(strain, fiducial, psd, time_shift, phase_shift, bin_blocks, bin_owner):
    n_freq = lax.axis_size("freq")
    me = lax.axis_index("freq")
    rows, width = psd.shape
    blocks = width // LANES
    bins = bin_blocks.shape[1]
    pair = bins // n_freq
    most = 2 * blocks // bins
    span = 2 * most

    strain_v = strain.reshape(2, rows, blocks, LANES).transpose(0, 2, 1, 3).reshape(2, blocks * rows, LANES)
    fid_v = fiducial.reshape(2, rows, blocks, LANES).transpose(0, 2, 1, 3).reshape(2, blocks * rows, LANES)
    psd_v = psd.reshape(rows, blocks, LANES).transpose(1, 0, 2).reshape(blocks * rows, LANES)

    up = [(i, i + 1) for i in range(n_freq - 1)]
    down = [(i + 1, i) for i in range(n_freq - 1)]
    halo = jnp.stack([lax.ppermute(psd_v[-8:], "freq", up), lax.ppermute(psd_v[:8], "freq", down)])

    rate = two_pi * time_shift
    total = width * n_freq
    table_blocks = TABLE // rows
    inside = jnp.arange(table_blocks * LANES, dtype=jnp.int32).astype(jnp.float32).reshape(table_blocks, 1, LANES) / total
    inside = (rate[None, :, None] * inside).reshape(TABLE, LANES)
    first = me * width + jnp.arange(blocks // table_blocks, dtype=jnp.int32) * (table_blocks * LANES)
    outer = rate[None, :] * (first.astype(jnp.float32) / total)[:, None] + phase_shift[None, :]
    spread = lambda v: jnp.broadcast_to(jnp.tile(v, (1, 8 // rows))[:, :, None], (v.shape[0], 8, LANES))
    real, imag, power = heterodyne(
        strain_v, fid_v, psd_v, halo,
        jnp.cos(inside), jnp.sin(inside), spread(jnp.cos(outer)), spread(jnp.sin(outer)),
    )

    position = jnp.arange(bins, dtype=jnp.int32)
    earlier = (position[None, :] < position[:, None])[None]
    same = bin_owner[:, :, None] == bin_owner[:, None, :]
    both = jnp.logical_and(same, earlier)
    starts = jnp.sum(jnp.where(earlier, bin_blocks[:, None, :], 0), axis=2)
    ranks = jnp.sum(both.astype(jnp.int32), axis=2)
    offsets = jnp.sum(jnp.where(both, bin_blocks[:, None, :], 0), axis=2)
    at_me = lambda a: lax.dynamic_index_in_dim(a, me, 0, keepdims=False)
    my_start, my_len, my_owner, my_off, my_rank = map(at_me, (starts, bin_blocks, bin_owner, offsets, ranks))

    pick = lambda key, values: jnp.sum(
        jnp.where(key[None, :] == position[:, None], values[None, :], 0), axis=1
    )
    by_step = (my_owner ^ me) * pair + my_rank
    send_start, send_len, send_off = (pick(by_step, v) for v in (my_start, my_len, my_off))
    peers = jnp.arange(n_freq, dtype=jnp.int32) ^ me
    to_me = jnp.logical_and(
        (bin_owner == me)[:, None, :], ranks[:, None, :] == jnp.arange(pair, dtype=jnp.int32)[None, :, None]
    )
    to_me = jnp.logical_and(to_me[None], (peers[:, None] == jnp.arange(n_freq)[None, :])[:, :, None, None])
    in_len = jnp.sum(jnp.where(to_me, bin_blocks[None, :, None, :], 0), axis=(1, 3)).reshape(-1)
    in_off = jnp.sum(jnp.where(to_me, offsets[None, :, None, :], 0), axis=(1, 3)).reshape(-1)
    where = jnp.stack([me // 2, me % 2]).astype(jnp.int32)

    steps = list(range(n_freq // 2, n_freq)) + list(range(1, n_freq // 2))
    got = []
    for values in (real, imag):
        packed = pack(send_start, send_len, send_off, values.reshape(blocks, rows, LANES), n_freq, span)
        here = {0: packed[0]}
        for s in steps:
            here[s] = lax.ppermute(packed[s], "freq", [(i, i ^ s) for i in range(n_freq)])
        got.append(here)

    my_slot = my_owner * pair + my_rank
    slot_first, slot_len = pick(my_slot, my_start), pick(my_slot, my_len)
    flat, tilted = bin_sums(rows, real, imag, power, jnp.tile(slot_first, rows)[None], jnp.tile(slot_len, rows)[None])
    flat = flat[:6].reshape(3, 2, rows, bins)
    plain = flat[:, 0]
    slope = flat[:, 1] + tilted[:6].reshape(3, 2, rows, bins)[:, 0]
    local_summary = jnp.concatenate(
        [plain[:2] * ratio_scale, slope[:2] * ratio_scale, plain[2:] * power_scale, slope[2:] * power_scale]
    )
    summary = lax.all_to_all(local_summary, "freq", split_axis=2, concat_axis=2, tiled=True)

    moved = None
    half = n_freq // 4
    units = list(range(half)) + list(range(half, 2 * half))
    for part in range(2):
        for unit in units:
            moved = unpack(
                part, unit, where, in_len, in_off, got[part][2 * unit], got[part][2 * unit + 1],
                moved, bins, pair, most,
            )
    return (moved, summary)


def solution(mesh):
    return jax.shard_map(
        local,
        mesh=mesh,
        in_specs=(
            P(None, "tmpl", "freq"),
            P(None, "tmpl", "freq"),
            P("tmpl", "freq"),
            P("tmpl"),
            P("tmpl"),
            P(),
            P(),
        ),
        out_specs=(P(None, "tmpl", "freq", None), P(None, "tmpl", "freq")),
        check_vma=False,
    )
```

```python
import functools
import math

import jax
import jax.numpy as jnp
from jax import lax
from jax.experimental import pallas as pl
from jax.experimental.pallas import tpu as pltpu
from jax.sharding import PartitionSpec as P


two_pi = 2.0 * math.pi
ratio_scale = 1.0 / 64.0
power_scale = 1.0 / 2048.0
LANES = 128
SUB = 32
TABLE = 256


def het_kernel(strain, fid, psd, prev, nxt, halo, cos_t, sin_t, cos_s, sin_s, real, imag, power, pad):
    rows = psd.shape[0]
    step, last = pl.program_id(0), pl.num_programs(0) - 1
    pad[8 : 8 + rows] = psd[...]
    pad[0:8] = jnp.where(step == 0, halo[0], prev[...])
    pad[8 + rows : 16 + rows] = jnp.where(step == last, halo[1], nxt[...])
    lane = lax.broadcasted_iota(jnp.int32, (SUB, LANES), 1)
    fold = (SUB // 8, 8, LANES)

    for outer in range(rows // TABLE):
        cs, ss = cos_s[outer][None], sin_s[outer][None]

        def inner(i, carry, outer=outer, cs=cs, ss=ss):
            off = pl.multiple_of(i * SUB, SUB)
            at = pl.multiple_of(outer * TABLE + i * SUB, SUB)
            x = pad[pl.ds(at + 8, SUB)]
            before = pltpu.roll(jnp.where(lane == LANES - 1, pad[pl.ds(at + 4, SUB)], x), 1, 1)
            after = pltpu.roll(jnp.where(lane == 0, pad[pl.ds(at + 12, SUB)], x), LANES - 1, 1)
            weight = 1.0 / (0.25 * (before + 2.0 * x + after))
            ct = cos_t[pl.ds(off, SUB)].reshape(fold)
            st = sin_t[pl.ds(off, SUB)].reshape(fold)
            cosine = (ct * cs - st * ss).reshape(SUB, LANES)
            sine = (st * cs + ct * ss).reshape(SUB, LANES)
            s_re = strain[0, pl.ds(at, SUB)].astype(jnp.float32)
            s_im = strain[1, pl.ds(at, SUB)].astype(jnp.float32)
            f_re = fid[0, pl.ds(at, SUB)].astype(jnp.float32)
            f_im = fid[1, pl.ds(at, SUB)].astype(jnp.float32)
            cross_re = s_re * f_re + s_im * f_im
            cross_im = s_im * f_re - s_re * f_im
            real[pl.ds(at, SUB)] = (weight * (cross_re * cosine + cross_im * sine)).astype(jnp.bfloat16)
            imag[pl.ds(at, SUB)] = (weight * (cross_im * cosine - cross_re * sine)).astype(jnp.bfloat16)
            power[pl.ds(at, SUB)] = (weight * (f_re * f_re + f_im * f_im)).astype(jnp.bfloat16)
            return carry

        lax.fori_loop(0, TABLE // SUB, inner, 0, unroll=2)


def heterodyne(strain, fid, psd, halo, cos_t, sin_t, cos_s, sin_s):
    total = psd.shape[0]
    rows = min(1024, total)
    steps = total // rows
    per = rows // 8
    return pl.pallas_call(
        het_kernel,
        grid=(steps,),
        in_specs=[
            pl.BlockSpec((2, rows, LANES), lambda i: (0, i, 0)),
            pl.BlockSpec((2, rows, LANES), lambda i: (0, i, 0)),
            pl.BlockSpec((rows, LANES), lambda i: (i, 0)),
            pl.BlockSpec((8, LANES), lambda i: (jnp.maximum(i * per - 1, 0), 0)),
            pl.BlockSpec((8, LANES), lambda i: (jnp.minimum((i + 1) * per, steps * per - 1), 0)),
            pl.BlockSpec((2, 8, LANES), lambda i: (0, 0, 0)),
            pl.BlockSpec((TABLE, LANES), lambda i: (0, 0)),
            pl.BlockSpec((TABLE, LANES), lambda i: (0, 0)),
            pl.BlockSpec((rows // TABLE, 8, LANES), lambda i: (i, 0, 0)),
            pl.BlockSpec((rows // TABLE, 8, LANES), lambda i: (i, 0, 0)),
        ],
        out_specs=[pl.BlockSpec((rows, LANES), lambda i: (i, 0))] * 3,
        out_shape=[jax.ShapeDtypeStruct((total, LANES), jnp.bfloat16)] * 3,
        scratch_shapes=[pltpu.VMEM((rows + 16, LANES), jnp.float32)],
        cost_estimate=pl.CostEstimate(flops=60 * total * LANES, bytes_accessed=18 * total * LANES, transcendentals=0),
        name="heterodyne",
    )(strain, fid, psd, psd, psd, halo, cos_t, sin_t, cos_s, sin_s)


def sums_kernel(tmpl_rows, real, imag, power, first, length, flat, tilted):
    rows = real.shape[0]
    cols = flat.shape[1]
    step = pl.program_id(0)
    row = lax.broadcasted_iota(jnp.int32, (8, LANES), 0)
    col = lax.broadcasted_iota(jnp.int32, (8, LANES), 1).astype(jnp.float32)
    lanes = jnp.zeros((8, rows), jnp.float32)
    for q, values in enumerate((real, imag, power)):
        w = jnp.where(row == 2 * q, 1.0, jnp.where(row == 2 * q + 1, (col + 0.5) / 128.0, 0.0))
        lanes += lax.dot_general(
            w.astype(jnp.bfloat16), values[...], (((1,), (1,)), ((), ())),
            preferred_element_type=jnp.float32,
        )
    index = lax.broadcasted_iota(jnp.int32, (rows, cols), 0)
    slot_row = lax.broadcasted_iota(jnp.int32, (rows, cols), 1) // (cols // tmpl_rows)
    rel = step * (rows // tmpl_rows) + index // tmpl_rows - first[...]
    live = (index % tmpl_rows == slot_row) & (rel >= 0) & (rel < length[...])
    mask = jnp.where(live, 1.0, 0.0)
    tilt = jnp.where(live, rel.astype(jnp.float32) - 0.5 * length[...].astype(jnp.float32), 0.0)

    @pl.when(step == 0)
    def _():
        flat[...] = jnp.zeros_like(flat)
        tilted[...] = jnp.zeros_like(tilted)

    dot = functools.partial(jnp.dot, precision=lax.Precision.HIGHEST, preferred_element_type=jnp.float32)
    flat[...] += dot(lanes, mask)
    tilted[...] += dot(lanes, tilt)


def bin_sums(tmpl_rows, real, imag, power, first, length):
    total = real.shape[0]
    rows = min(1024, total)
    cols = first.shape[1]
    block = pl.BlockSpec((rows, LANES), lambda i: (i, 0))
    table = pl.BlockSpec((1, cols), lambda i: (0, 0))
    return pl.pallas_call(
        functools.partial(sums_kernel, tmpl_rows),
        grid=(total // rows,),
        in_specs=[block, block, block, table, table],
        out_specs=[pl.BlockSpec((8, cols), lambda i: (0, 0))] * 2,
        out_shape=[jax.ShapeDtypeStruct((8, cols), jnp.float32)] * 2,
        cost_estimate=pl.CostEstimate(flops=200 * total * LANES, bytes_accessed=6 * total * LANES, transcendentals=0),
        name="sums",
    )(real, imag, power, first, length)


def pack_kernel(lengths, owners, prod, *rest):
    *packed, first, size, offset, count, filled, sem = rest
    groups, bins = lengths.shape
    pair = bins // groups
    me = lax.axis_index("freq")
    span = packed[0].shape[0]

    def clear(p, carry):
        count[p] = 0
        filled[p] = 0
        return carry

    lax.fori_loop(0, groups, clear, 0)

    def place(j, start):
        step = owners[me, j] ^ me
        n = lengths[me, j]
        slot = step * pair + count[step]
        first[slot] = start
        size[slot] = n
        offset[slot] = filled[step]
        count[step] = count[step] + 1
        filled[step] = filled[step] + n
        return start + n

    lax.fori_loop(0, bins, place, jnp.int32(0))

    order = list(range(groups // 2, groups)) + list(range(groups // 2))
    for step in order:
        for rank in range(pair):
            j = step * pair + rank
            n = size[j]
            pltpu.make_async_copy(
                prod.at[pl.ds(first[j], n)], packed[step].at[pl.ds(offset[j], n)], sem.at[step]
            ).start()
    for step in order:
        pltpu.make_async_copy(prod.at[pl.ds(0, span)], packed[step], sem.at[step]).wait()


def pack(lengths, owners, prod, span):
    groups, bins = lengths.shape
    shape = jax.ShapeDtypeStruct((span,) + prod.shape[1:], jnp.bfloat16)
    return pl.pallas_call(
        pack_kernel,
        grid_spec=pltpu.PrefetchScalarGridSpec(
            num_scalar_prefetch=2,
            in_specs=[pl.BlockSpec(memory_space=pltpu.VMEM)],
            out_specs=[pl.BlockSpec(memory_space=pl.ANY)] * groups,
            scratch_shapes=[pltpu.SMEM((bins,), jnp.int32)] * 3
            + [pltpu.SMEM((groups,), jnp.int32)] * 2
            + [pltpu.SemaphoreType.DMA((groups,))],
        ),
        out_shape=[shape] * groups,
        cost_estimate=pl.CostEstimate(flops=0, bytes_accessed=4 * prod.size, transcendentals=0),
        name="pack",
    )(lengths, owners, prod)


def unpack_kernel(chunk, pair, unit, where, lengths, offsets, near, far, *rest):
    out, work = rest[-2:]
    m0 = pl.program_id(0) * chunk
    span, rows = near.shape[0], near.shape[1]
    slots = out.shape[2]
    for half, got in enumerate((near, far)):
        base_slot = (where[1] ^ half) * pair
        for rank in range(pair):
            j = (2 * unit + half) * pair + rank
            n = lengths[j] - m0
            base = offsets[j] + m0
            lane = base_slot + rank

            @pl.when(n >= chunk)
            def _(got=got, base=base, lane=lane):
                for m in range(chunk):
                    work[m, pl.ds(lane, rows, stride=slots)] = got[base + m].astype(jnp.float32)

            @pl.when(jnp.logical_and(n > 0, n < chunk))
            def _(got=got, n=n, base=base, lane=lane):
                for m in range(chunk):
                    value = got[jnp.minimum(base + m, span - 1)].astype(jnp.float32)
                    value = jnp.where(m < n, value, 0.0)
                    work[m, pl.ds(lane, rows, stride=slots)] = value

            @pl.when(n <= 0)
            def _(lane=lane):
                for m in range(chunk):
                    work[m, pl.ds(lane, rows, stride=slots)] = jnp.zeros((rows, LANES), jnp.float32)

    for m in range(chunk):
        for r in range(rows):
            out[0, r, :, m * LANES : (m + 1) * LANES] = work[m, r * slots : (r + 1) * slots].astype(jnp.bfloat16)


def unpack(part, unit, where, lengths, offsets, near, far, dest, bins, pair, most):
    span, rows, _ = near.shape
    slots = 2 * pair
    chunk = min(16, most)
    whole = pl.BlockSpec((span, rows, LANES), lambda m, *_: (0, 0, 0))
    extra = [] if dest is None else [dest]
    size = rows * slots * most * LANES
    return pl.pallas_call(
        functools.partial(unpack_kernel, chunk, pair, unit),
        grid_spec=pltpu.PrefetchScalarGridSpec(
            num_scalar_prefetch=3,
            grid=(most // chunk,),
            in_specs=[whole, whole] + [pl.BlockSpec(memory_space=pl.ANY)] * len(extra),
            out_specs=pl.BlockSpec(
                (1, rows, slots, chunk * LANES), lambda m, w, *_: (part, 0, w[0] ^ unit, m)
            ),
            scratch_shapes=[pltpu.VMEM((chunk, rows * slots, LANES), jnp.float32)],
        ),
        out_shape=jax.ShapeDtypeStruct((2, rows, bins, most * LANES), jnp.bfloat16),
        input_output_aliases={5: 0} if extra else {},
        cost_estimate=pl.CostEstimate(flops=8 * size, bytes_accessed=3 * size, transcendentals=0),
        name="unpack",
    )(where, lengths, offsets, near, far, *extra)


def local(strain, fiducial, psd, time_shift, phase_shift, bin_blocks, bin_owner):
    n_freq = lax.axis_size("freq")
    me = lax.axis_index("freq")
    rows, width = psd.shape
    blocks = width // LANES
    bins = bin_blocks.shape[1]
    pair = bins // n_freq
    most = 2 * blocks // bins
    span = 2 * most

    strain_v = strain.reshape(2, rows, blocks, LANES).transpose(0, 2, 1, 3).reshape(2, blocks * rows, LANES)
    fid_v = fiducial.reshape(2, rows, blocks, LANES).transpose(0, 2, 1, 3).reshape(2, blocks * rows, LANES)
    psd_v = psd.reshape(rows, blocks, LANES).transpose(1, 0, 2).reshape(blocks * rows, LANES)

    up = [(i, i + 1) for i in range(n_freq - 1)]
    down = [(i + 1, i) for i in range(n_freq - 1)]
    halo = jnp.stack([lax.ppermute(psd_v[-8:], "freq", up), lax.ppermute(psd_v[:8], "freq", down)])

    rate = two_pi * time_shift
    total = width * n_freq
    table_blocks = TABLE // rows
    inside = jnp.arange(table_blocks * LANES, dtype=jnp.int32).astype(jnp.float32).reshape(table_blocks, 1, LANES) / total
    inside = (rate[None, :, None] * inside).reshape(TABLE, LANES)
    first = me * width + jnp.arange(blocks // table_blocks, dtype=jnp.int32) * (table_blocks * LANES)
    outer = rate[None, :] * (first.astype(jnp.float32) / total)[:, None] + phase_shift[None, :]
    spread = lambda v: jnp.broadcast_to(jnp.tile(v, (1, 8 // rows))[:, :, None], (v.shape[0], 8, LANES))
    real, imag, power = heterodyne(
        strain_v, fid_v, psd_v, halo,
        jnp.cos(inside), jnp.sin(inside), spread(jnp.cos(outer)), spread(jnp.sin(outer)),
    )

    steps = list(range(n_freq // 2, n_freq)) + list(range(1, n_freq // 2))
    got = []
    for values in (real, imag):
        packed = pack(bin_blocks, bin_owner, values.reshape(blocks, rows, LANES), span)
        here = {0: packed[0]}
        for s in steps:
            here[s] = lax.ppermute(packed[s], "freq", [(i, i ^ s) for i in range(n_freq)])
        got.append(here)

    bin_blocks, bin_owner, got[1][0] = lax.optimization_barrier((bin_blocks, bin_owner, got[1][0]))
    position = jnp.arange(bins, dtype=jnp.int32)
    earlier = (position[None, :] < position[:, None])[None]
    same = bin_owner[:, :, None] == bin_owner[:, None, :]
    both = jnp.logical_and(same, earlier)
    starts = jnp.sum(jnp.where(earlier, bin_blocks[:, None, :], 0), axis=2)
    ranks = jnp.sum(both.astype(jnp.int32), axis=2)
    offsets = jnp.sum(jnp.where(both, bin_blocks[:, None, :], 0), axis=2)
    at_me = lambda a: lax.dynamic_index_in_dim(a, me, 0, keepdims=False)
    my_start, my_len, my_owner, _, my_rank = map(at_me, (starts, bin_blocks, bin_owner, offsets, ranks))

    pick = lambda key, values: jnp.sum(
        jnp.where(key[None, :] == position[:, None], values[None, :], 0), axis=1
    )
    peers = jnp.arange(n_freq, dtype=jnp.int32) ^ me
    to_me = jnp.logical_and(
        (bin_owner == me)[:, None, :], ranks[:, None, :] == jnp.arange(pair, dtype=jnp.int32)[None, :, None]
    )
    to_me = jnp.logical_and(to_me[None], (peers[:, None] == jnp.arange(n_freq)[None, :])[:, :, None, None])
    in_len = jnp.sum(jnp.where(to_me, bin_blocks[None, :, None, :], 0), axis=(1, 3)).reshape(-1)
    in_off = jnp.sum(jnp.where(to_me, offsets[None, :, None, :], 0), axis=(1, 3)).reshape(-1)
    where = jnp.stack([me // 2, me % 2]).astype(jnp.int32)

    my_slot = my_owner * pair + my_rank
    slot_first, slot_len = pick(my_slot, my_start), pick(my_slot, my_len)
    flat, tilted = bin_sums(rows, real, imag, power, jnp.tile(slot_first, rows)[None], jnp.tile(slot_len, rows)[None])
    flat = flat[:6].reshape(3, 2, rows, bins)
    plain = flat[:, 0]
    slope = flat[:, 1] + tilted[:6].reshape(3, 2, rows, bins)[:, 0]
    local_summary = jnp.concatenate(
        [plain[:2] * ratio_scale, slope[:2] * ratio_scale, plain[2:] * power_scale, slope[2:] * power_scale]
    )
    summary = lax.all_to_all(local_summary, "freq", split_axis=2, concat_axis=2, tiled=True)

    moved = None
    half = n_freq // 4
    units = list(range(half)) + list(range(half, 2 * half))
    for part in range(2):
        for unit in units:
            moved = unpack(
                part, unit, where, in_len, in_off, got[part][2 * unit], got[part][2 * unit + 1],
                moved, bins, pair, most,
            )
    return (moved, summary)


def solution(mesh):
    return jax.shard_map(
        local,
        mesh=mesh,
        in_specs=(
            P(None, "tmpl", "freq"),
            P(None, "tmpl", "freq"),
            P("tmpl", "freq"),
            P("tmpl"),
            P("tmpl"),
            P(),
            P(),
        ),
        out_specs=(P(None, "tmpl", "freq", None), P(None, "tmpl", "freq")),
        check_vma=False,
    )
```

```python
import functools
import math

import jax
import jax.numpy as jnp
from jax import lax
from jax.experimental import pallas as pl
from jax.experimental.pallas import tpu as pltpu
from jax.sharding import PartitionSpec as P


two_pi = 2.0 * math.pi
ratio_scale = 1.0 / 64.0
power_scale = 1.0 / 2048.0
LANES = 128
SUB = 32
TABLE = 256


def het_kernel(strain, fid, psd, prev, nxt, halo, cos_t, sin_t, cos_s, sin_s, real, imag, power, pad):
    rows = psd.shape[0]
    step, last = pl.program_id(0), pl.num_programs(0) - 1
    pad[8 : 8 + rows] = psd[...]
    pad[0:8] = jnp.where(step == 0, halo[0], prev[...])
    pad[8 + rows : 16 + rows] = jnp.where(step == last, halo[1], nxt[...])
    lane = lax.broadcasted_iota(jnp.int32, (SUB, LANES), 1)
    fold = (SUB // 8, 8, LANES)

    for outer in range(rows // TABLE):
        cs, ss = cos_s[outer][None], sin_s[outer][None]

        def inner(i, carry, outer=outer, cs=cs, ss=ss):
            off = pl.multiple_of(i * SUB, SUB)
            at = pl.multiple_of(outer * TABLE + i * SUB, SUB)
            x = pad[pl.ds(at + 8, SUB)]
            before = pltpu.roll(jnp.where(lane == LANES - 1, pad[pl.ds(at + 4, SUB)], x), 1, 1)
            after = pltpu.roll(jnp.where(lane == 0, pad[pl.ds(at + 12, SUB)], x), LANES - 1, 1)
            weight = 1.0 / (0.25 * (before + 2.0 * x + after))
            ct = cos_t[pl.ds(off, SUB)].reshape(fold)
            st = sin_t[pl.ds(off, SUB)].reshape(fold)
            cosine = (ct * cs - st * ss).reshape(SUB, LANES)
            sine = (st * cs + ct * ss).reshape(SUB, LANES)
            s_re = strain[0, pl.ds(at, SUB)].astype(jnp.float32)
            s_im = strain[1, pl.ds(at, SUB)].astype(jnp.float32)
            f_re = fid[0, pl.ds(at, SUB)].astype(jnp.float32)
            f_im = fid[1, pl.ds(at, SUB)].astype(jnp.float32)
            cross_re = s_re * f_re + s_im * f_im
            cross_im = s_im * f_re - s_re * f_im
            real[pl.ds(at, SUB)] = (weight * (cross_re * cosine + cross_im * sine)).astype(jnp.bfloat16)
            imag[pl.ds(at, SUB)] = (weight * (cross_im * cosine - cross_re * sine)).astype(jnp.bfloat16)
            power[pl.ds(at, SUB)] = (weight * (f_re * f_re + f_im * f_im)).astype(jnp.bfloat16)
            return carry

        lax.fori_loop(0, TABLE // SUB, inner, 0, unroll=2)


def heterodyne(strain, fid, psd, halo, cos_t, sin_t, cos_s, sin_s):
    total = psd.shape[0]
    rows = min(1024, total)
    steps = total // rows
    per = rows // 8
    return pl.pallas_call(
        het_kernel,
        grid=(steps,),
        in_specs=[
            pl.BlockSpec((2, rows, LANES), lambda i: (0, i, 0)),
            pl.BlockSpec((2, rows, LANES), lambda i: (0, i, 0)),
            pl.BlockSpec((rows, LANES), lambda i: (i, 0)),
            pl.BlockSpec((8, LANES), lambda i: (jnp.maximum(i * per - 1, 0), 0)),
            pl.BlockSpec((8, LANES), lambda i: (jnp.minimum((i + 1) * per, steps * per - 1), 0)),
            pl.BlockSpec((2, 8, LANES), lambda i: (0, 0, 0)),
            pl.BlockSpec((TABLE, LANES), lambda i: (0, 0)),
            pl.BlockSpec((TABLE, LANES), lambda i: (0, 0)),
            pl.BlockSpec((rows // TABLE, 8, LANES), lambda i: (i, 0, 0)),
            pl.BlockSpec((rows // TABLE, 8, LANES), lambda i: (i, 0, 0)),
        ],
        out_specs=[pl.BlockSpec((rows, LANES), lambda i: (i, 0))] * 3,
        out_shape=[jax.ShapeDtypeStruct((total, LANES), jnp.bfloat16)] * 3,
        scratch_shapes=[pltpu.VMEM((rows + 16, LANES), jnp.float32)],
        cost_estimate=pl.CostEstimate(flops=60 * total * LANES, bytes_accessed=18 * total * LANES, transcendentals=0),
        name="heterodyne",
    )(strain, fid, psd, psd, psd, halo, cos_t, sin_t, cos_s, sin_s)


def sums_kernel(tmpl_rows, real, imag, power, first, length, flat, tilted):
    rows = real.shape[0]
    cols = flat.shape[1]
    step = pl.program_id(0)
    row = lax.broadcasted_iota(jnp.int32, (8, LANES), 0)
    col = lax.broadcasted_iota(jnp.int32, (8, LANES), 1).astype(jnp.float32)
    lanes = jnp.zeros((8, rows), jnp.float32)
    for q, values in enumerate((real, imag, power)):
        w = jnp.where(row == 2 * q, 1.0, jnp.where(row == 2 * q + 1, (col + 0.5) / 128.0, 0.0))
        lanes += lax.dot_general(
            w.astype(jnp.bfloat16), values[...], (((1,), (1,)), ((), ())),
            preferred_element_type=jnp.float32,
        )
    index = lax.broadcasted_iota(jnp.int32, (rows, cols), 0)
    slot_row = lax.broadcasted_iota(jnp.int32, (rows, cols), 1) // (cols // tmpl_rows)
    rel = step * (rows // tmpl_rows) + index // tmpl_rows - first[...]
    live = (index % tmpl_rows == slot_row) & (rel >= 0) & (rel < length[...])
    mask = jnp.where(live, 1.0, 0.0)
    tilt = jnp.where(live, rel.astype(jnp.float32) - 0.5 * length[...].astype(jnp.float32), 0.0)

    @pl.when(step == 0)
    def _():
        flat[...] = jnp.zeros_like(flat)
        tilted[...] = jnp.zeros_like(tilted)

    dot = functools.partial(jnp.dot, precision=lax.Precision.HIGHEST, preferred_element_type=jnp.float32)
    flat[...] += dot(lanes, mask)
    tilted[...] += dot(lanes, tilt)


def bin_sums(tmpl_rows, real, imag, power, first, length):
    total = real.shape[0]
    rows = min(1024, total)
    cols = first.shape[1]
    block = pl.BlockSpec((rows, LANES), lambda i: (i, 0))
    table = pl.BlockSpec((1, cols), lambda i: (0, 0))
    return pl.pallas_call(
        functools.partial(sums_kernel, tmpl_rows),
        grid=(total // rows,),
        in_specs=[block, block, block, table, table],
        out_specs=[pl.BlockSpec((8, cols), lambda i: (0, 0))] * 2,
        out_shape=[jax.ShapeDtypeStruct((8, cols), jnp.float32)] * 2,
        cost_estimate=pl.CostEstimate(flops=200 * total * LANES, bytes_accessed=6 * total * LANES, transcendentals=0),
        name="sums",
    )(real, imag, power, first, length)


def pack_kernel(lengths, owners, prod, *rest):
    *packed, first, size, offset, count, filled, sem = rest
    groups, bins = lengths.shape
    pair = bins // groups
    me = lax.axis_index("freq")
    span = packed[0].shape[0]

    def clear(p, carry):
        count[p] = 0
        filled[p] = 0
        return carry

    lax.fori_loop(0, groups, clear, 0)

    def place(j, start):
        step = owners[me, j] ^ me
        n = lengths[me, j]
        slot = step * pair + count[step]
        first[slot] = start
        size[slot] = n
        offset[slot] = filled[step]
        count[step] = count[step] + 1
        filled[step] = filled[step] + n
        return start + n

    lax.fori_loop(0, bins, place, jnp.int32(0))

    order = list(range(groups // 2, groups)) + list(range(groups // 2))
    for step in order:
        for rank in range(pair):
            j = step * pair + rank
            n = size[j]
            pltpu.make_async_copy(
                prod.at[pl.ds(first[j], n)], packed[step].at[pl.ds(offset[j], n)], sem.at[step]
            ).start()
    for step in order:
        pltpu.make_async_copy(prod.at[pl.ds(0, span)], packed[step], sem.at[step]).wait()


def pack(lengths, owners, prod, span):
    groups, bins = lengths.shape
    shape = jax.ShapeDtypeStruct((span,) + prod.shape[1:], jnp.bfloat16)
    return pl.pallas_call(
        pack_kernel,
        grid_spec=pltpu.PrefetchScalarGridSpec(
            num_scalar_prefetch=2,
            in_specs=[pl.BlockSpec(memory_space=pltpu.VMEM)],
            out_specs=[pl.BlockSpec(memory_space=pl.ANY)] * groups,
            scratch_shapes=[pltpu.SMEM((bins,), jnp.int32)] * 3
            + [pltpu.SMEM((groups,), jnp.int32)] * 2
            + [pltpu.SemaphoreType.DMA((groups,))],
        ),
        out_shape=[shape] * groups,
        cost_estimate=pl.CostEstimate(flops=0, bytes_accessed=4 * prod.size, transcendentals=0),
        name="pack",
    )(lengths, owners, prod)


def unpack_kernel(chunk, pair, unit, where, lengths, offsets, near, far, *rest):
    out, work = rest[-2:]
    span, rows = near.shape[0], near.shape[1]
    slots = out.shape[2]
    pieces = out.shape[3] // (chunk * LANES)

    def one(piece, carry):
        m0 = (pl.program_id(0) * pieces + piece) * chunk
        for half, got in enumerate((near, far)):
            base_slot = (where[1] ^ half) * pair
            for rank in range(pair):
                j = (2 * unit + half) * pair + rank
                n = lengths[j] - m0
                base = offsets[j] + m0
                lane = base_slot + rank

                @pl.when(n >= chunk)
                def _(got=got, base=base, lane=lane):
                    for m in range(chunk):
                        work[m, pl.ds(lane, rows, stride=slots)] = got[base + m].astype(jnp.float32)

                @pl.when(jnp.logical_and(n > 0, n < chunk))
                def _(got=got, n=n, base=base, lane=lane):
                    for m in range(chunk):
                        value = got[jnp.minimum(base + m, span - 1)].astype(jnp.float32)
                        value = jnp.where(m < n, value, 0.0)
                        work[m, pl.ds(lane, rows, stride=slots)] = value

                @pl.when(n <= 0)
                def _(lane=lane):
                    for m in range(chunk):
                        work[m, pl.ds(lane, rows, stride=slots)] = jnp.zeros((rows, LANES), jnp.float32)

        for m in range(chunk):
            for r in range(rows):
                out[0, r, :, pl.ds(pl.multiple_of((piece * chunk + m) * LANES, LANES), LANES)] = work[m, r * slots : (r + 1) * slots].astype(jnp.bfloat16)
        return carry

    lax.fori_loop(0, pieces, one, 0)


def unpack(part, unit, where, lengths, offsets, near, far, dest, bins, pair, most):
    span, rows, _ = near.shape
    slots = 2 * pair
    chunk = min(16, most)
    wide = min(64, most)
    whole = pl.BlockSpec((span, rows, LANES), lambda m, *_: (0, 0, 0))
    extra = [] if dest is None else [dest]
    size = rows * slots * most * LANES
    return pl.pallas_call(
        functools.partial(unpack_kernel, chunk, pair, unit),
        grid_spec=pltpu.PrefetchScalarGridSpec(
            num_scalar_prefetch=3,
            grid=(most // wide,),
            in_specs=[whole, whole] + [pl.BlockSpec(memory_space=pl.ANY)] * len(extra),
            out_specs=pl.BlockSpec(
                (1, rows, slots, wide * LANES), lambda m, w, *_: (part, 0, w[0] ^ unit, m)
            ),
            scratch_shapes=[pltpu.VMEM((chunk, rows * slots, LANES), jnp.float32)],
        ),
        out_shape=jax.ShapeDtypeStruct((2, rows, bins, most * LANES), jnp.bfloat16),
        input_output_aliases={5: 0} if extra else {},
        compiler_params=pltpu.CompilerParams(vmem_limit_bytes=60 * 1024 * 1024),
        cost_estimate=pl.CostEstimate(flops=8 * size, bytes_accessed=3 * size, transcendentals=0),
        name="unpack",
    )(where, lengths, offsets, near, far, *extra)


def local(strain, fiducial, psd, time_shift, phase_shift, bin_blocks, bin_owner):
    n_freq = lax.axis_size("freq")
    me = lax.axis_index("freq")
    rows, width = psd.shape
    blocks = width // LANES
    bins = bin_blocks.shape[1]
    pair = bins // n_freq
    most = 2 * blocks // bins
    span = 2 * most

    strain_v = strain.reshape(2, rows, blocks, LANES).transpose(0, 2, 1, 3).reshape(2, blocks * rows, LANES)
    fid_v = fiducial.reshape(2, rows, blocks, LANES).transpose(0, 2, 1, 3).reshape(2, blocks * rows, LANES)
    psd_v = psd.reshape(rows, blocks, LANES).transpose(1, 0, 2).reshape(blocks * rows, LANES)

    up = [(i, i + 1) for i in range(n_freq - 1)]
    down = [(i + 1, i) for i in range(n_freq - 1)]
    halo = jnp.stack([lax.ppermute(psd_v[-8:], "freq", up), lax.ppermute(psd_v[:8], "freq", down)])

    rate = two_pi * time_shift
    total = width * n_freq
    table_blocks = TABLE // rows
    inside = jnp.arange(table_blocks * LANES, dtype=jnp.int32).astype(jnp.float32).reshape(table_blocks, 1, LANES) / total
    inside = (rate[None, :, None] * inside).reshape(TABLE, LANES)
    first = me * width + jnp.arange(blocks // table_blocks, dtype=jnp.int32) * (table_blocks * LANES)
    outer = rate[None, :] * (first.astype(jnp.float32) / total)[:, None] + phase_shift[None, :]
    spread = lambda v: jnp.broadcast_to(jnp.tile(v, (1, 8 // rows))[:, :, None], (v.shape[0], 8, LANES))
    real, imag, power = heterodyne(
        strain_v, fid_v, psd_v, halo,
        jnp.cos(inside), jnp.sin(inside), spread(jnp.cos(outer)), spread(jnp.sin(outer)),
    )

    steps = list(range(n_freq // 2, n_freq)) + list(range(1, n_freq // 2))
    got = []
    for values in (real, imag):
        packed = pack(bin_blocks, bin_owner, values.reshape(blocks, rows, LANES), span)
        here = {0: packed[0]}
        for s in steps:
            here[s] = lax.ppermute(packed[s], "freq", [(i, i ^ s) for i in range(n_freq)])
        got.append(here)

    bin_blocks, bin_owner, got[0][0] = lax.optimization_barrier((bin_blocks, bin_owner, got[0][0]))
    position = jnp.arange(bins, dtype=jnp.int32)
    earlier = (position[None, :] < position[:, None])[None]
    same = bin_owner[:, :, None] == bin_owner[:, None, :]
    both = jnp.logical_and(same, earlier)
    starts = jnp.sum(jnp.where(earlier, bin_blocks[:, None, :], 0), axis=2)
    ranks = jnp.sum(both.astype(jnp.int32), axis=2)
    offsets = jnp.sum(jnp.where(both, bin_blocks[:, None, :], 0), axis=2)
    at_me = lambda a: lax.dynamic_index_in_dim(a, me, 0, keepdims=False)
    my_start, my_len, my_owner, _, my_rank = map(at_me, (starts, bin_blocks, bin_owner, offsets, ranks))

    pick = lambda key, values: jnp.sum(
        jnp.where(key[None, :] == position[:, None], values[None, :], 0), axis=1
    )
    peers = jnp.arange(n_freq, dtype=jnp.int32) ^ me
    to_me = jnp.logical_and(
        (bin_owner == me)[:, None, :], ranks[:, None, :] == jnp.arange(pair, dtype=jnp.int32)[None, :, None]
    )
    to_me = jnp.logical_and(to_me[None], (peers[:, None] == jnp.arange(n_freq)[None, :])[:, :, None, None])
    in_len = jnp.sum(jnp.where(to_me, bin_blocks[None, :, None, :], 0), axis=(1, 3)).reshape(-1)
    in_off = jnp.sum(jnp.where(to_me, offsets[None, :, None, :], 0), axis=(1, 3)).reshape(-1)
    where = jnp.stack([me // 2, me % 2]).astype(jnp.int32)

    my_slot = my_owner * pair + my_rank
    slot_first, slot_len = pick(my_slot, my_start), pick(my_slot, my_len)
    flat, tilted = bin_sums(rows, real, imag, power, jnp.tile(slot_first, rows)[None], jnp.tile(slot_len, rows)[None])
    flat = flat[:6].reshape(3, 2, rows, bins)
    plain = flat[:, 0]
    slope = flat[:, 1] + tilted[:6].reshape(3, 2, rows, bins)[:, 0]
    local_summary = jnp.concatenate(
        [plain[:2] * ratio_scale, slope[:2] * ratio_scale, plain[2:] * power_scale, slope[2:] * power_scale]
    )
    summary = lax.all_to_all(local_summary, "freq", split_axis=2, concat_axis=2, tiled=True)

    moved = None
    half = n_freq // 4
    units = list(range(half)) + list(range(half, 2 * half))
    for part in range(2):
        for unit in units:
            moved = unpack(
                part, unit, where, in_len, in_off, got[part][2 * unit], got[part][2 * unit + 1],
                moved, bins, pair, most,
            )
    return (moved, summary)


def solution(mesh):
    return jax.shard_map(
        local,
        mesh=mesh,
        in_specs=(
            P(None, "tmpl", "freq"),
            P(None, "tmpl", "freq"),
            P("tmpl", "freq"),
            P("tmpl"),
            P("tmpl"),
            P(),
            P(),
        ),
        out_specs=(P(None, "tmpl", "freq", None), P(None, "tmpl", "freq")),
        check_vma=False,
    )
```
